32 devices in a mesh: row: 8 (over z, core), col: 4 (over y, x).
Axes of the slice: x: 2, y: 2, z: 4, core: 2. Of those that a mesh axis runs over, the one named last changes fastest.
Arguments:
- pivot_inverse: float32 [1024, 1024], P('row'), may hold values from -1 to 2, as said below
- panel: float32 [16, 1024, 1024], P('row', 'col'), may hold values from -1 to 1
- trailing: float32 [160, 1024, 1024], P('row', None, 'col'), may hold values from -6 to 6
- tile_list: int32 [160, 2], P('row'), may hold values from -1 to 15, as said below
Outputs:
- solved_panel: float32 [16, 1024, 1024], P('row', 'col')
- updated: float32 [160, 1024, 1024], P('row', None, 'col')
The draws below stay inside these ranges and needn't reach their ends.
Inputs may be any that keep to these rules, and one draw needn't show every extreme that they name: `pivot_inverse`: lower triangular, diagonal between 0.5 and 2. `tile_list`: slots t of group g are g * 20 to g * 20 + 19. Column 0 lies in 0 to 1; column 1 is a panel tile or -1 for an empty slot. The live slots of a group come first and name distinct pairs; each group in the first half of the groups holds exactly 6 live slots, each in the second half exactly 20. Empty slots hold 0 in column 0.
All inputs are finite; a program needn't handle non-finite values.
Results may differ from the reference program's by a relative error of at most 0.00007.
Values sent between devices are 32-bit elements; how exact they have to be, the bound alone decides.
A program may use at most 128 MiB of HBM per device.

```python
import math
import jax
import jax.numpy as jnp
from jax import lax

B = 1024
PAN_DEV = 2
TR_DEV = 20
LIGHT = 6
PANEL = 16
TRAIL = 160


def draw_pivot_inverse(key, part):
    first_key, second_key = jax.random.split(key)
    lower_part = jnp.tril(jax.random.normal(first_key, (B, B), jnp.float32), -1) * (0.6 / math.sqrt(B))
    diagonal = jnp.exp(jax.random.uniform(second_key, (B,), jnp.float32, math.log(0.5), math.log(2.0)))
    return (lower_part + jnp.diag(diagonal)).astype(jnp.float32)


def draw_tile_list(key, part):
    groups = TRAIL // TR_DEV
    options = PAN_DEV * PANEL
    group_keys = jax.random.split(jax.random.fold_in(key, 7), groups)
    shuffled = jax.vmap(lambda one_key: jax.random.permutation(one_key, options))(group_keys)[:, :TR_DEV]
    local_tile = shuffled // PANEL
    paired_tile = shuffled % PANEL
    slot_index = jnp.arange(TR_DEV)[None, :]
    group_index = jnp.arange(groups)[:, None]
    live_count = jnp.where(group_index >= groups // 2, TR_DEV, LIGHT)
    live_slot = slot_index < live_count
    local_tile = jnp.where(live_slot, local_tile, 0)
    paired_tile = jnp.where(live_slot, paired_tile, -1)
    return jnp.stack([local_tile, paired_tile], -1).reshape(TRAIL, 2).astype(jnp.int32)


def steps_of(rng, extent, pieces, least, high):
    level, own = 1.0, jax.random.fold_in(rng, 6)
    for axis_at, shards_of in pieces:
        steps = jnp.exp(jax.random.uniform(jax.random.fold_in(own, axis_at), (shards_of,), jnp.float32, least / len(pieces), high / len(pieces)))
        level = level * jnp.repeat(steps, extent[axis_at] // shards_of).reshape([-1 if axis == axis_at else 1 for axis in range(len(extent))])
    return level


def noise(own_key, shape, deviation, reach, cuts=(), kind=jnp.bfloat16):
    loudness = steps_of(own_key, shape, cuts, -0.22, 0.18) if cuts else 1.0
    values = jax.random.normal(own_key, shape, jnp.float32) * deviation * loudness
    return jnp.minimum(jnp.maximum(values, -reach), reach).astype(kind)


def setup_inputs(seed: int = 0) -> dict:
    seeds = jax.random.split(jax.random.key(seed), 5)
    pivot_inverse = draw_pivot_inverse(jax.random.fold_in(seeds[4], 71), 0)
    panel = noise(seeds[1], (PANEL, B, B), 0.18, 1.0, ((0, 8), (1, 4)), jnp.float32)
    trailing = noise(seeds[2], (TRAIL, B, B), 1.0, 6.0, ((0, 8), (2, 4)), jnp.float32)
    tile_list = draw_tile_list(jax.random.fold_in(seeds[4], 71), 0)
    return {"pivot_inverse": pivot_inverse, "panel": panel, "trailing": trailing, "tile_list": tile_list}


highest = lax.Precision.HIGHEST


def reference(pivot_inverse, panel, trailing, tile_list):
    solved = jnp.einsum("pak,jk->paj", panel, pivot_inverse, precision=highest)
    group_index = jnp.arange(TRAIL, dtype=jnp.int32) // TR_DEV
    row_tile = (group_index * PAN_DEV + tile_list[:, 0]).astype(jnp.int32)
    col_tile = jnp.maximum(tile_list[:, 1], 0).astype(jnp.int32)
    live_slot = tile_list[:, 1] >= 0

    def update_slot(packed):
        current, left_index, right_index, live_flag = packed
        product = jnp.einsum("ak,bk->ab", solved[left_index], solved[right_index], precision=highest)
        return current - jnp.where(live_flag, product, jnp.zeros_like(product))

    updated = lax.map(update_slot, (trailing, row_tile, col_tile, live_slot))
    return solved, updated
```

```python
import functools

import jax
import jax.numpy as jnp
from jax import lax
from jax.experimental import pallas as pl
from jax.experimental.pallas import tpu as pltpu
from jax.sharding import PartitionSpec as P

MESH = pl.DeviceIdType.MESH
LIGHT = 6
CHUNKS = 4
STAGES = 4
PIECES = (4, 1, 1, 2)
f32, bf16 = jnp.float32, jnp.bfloat16


def halves(x):
    hi = x.astype(bf16)
    return hi, (x - hi.astype(f32)).astype(bf16)


def dot_nt(a, b):
    return lax.dot_general(a, b, (((1,), (1,)), ((), ())), preferred_element_type=f32)


def dot_nn(a, b):
    return lax.dot_general(a, b, (((1,), (0,)), ((), ())), preferred_element_type=f32)


def table(index, values):
    found = jnp.int32(0)
    for at, value in enumerate(values):
        found = jnp.where(index == at, jnp.int32(value), found)
    return found


def over(lo, hi, act):
    def body(t, carry):
        act(t)
        return carry
    lax.fori_loop(lo, hi, body, 0)


def live_slots(row, rows, slots):
    return jnp.where(row < rows // 2, jnp.int32(min(LIGHT, slots)), jnp.int32(slots))


def gather_kernel(rows, cols, pivot, panel, trailing, tiles,
                  solved_buf, acc, q3_last, sl_last,
                  sl, q, factor, own_hi, own_lo, q3,
                  load_sem, in_sem,
                  lz_recv, lz_send, lr_recv, lr_send, ls_recv, ls_send,
                  row_recv, row_send, sib_recv, sib_send, q_recv, q_send):
    chips = rows // 2
    pan, height, order = panel.shape
    slots = trailing.shape[0]
    kc = order // CHUNKS
    block = order // chips
    far = cols // 2
    sl = [*sl, sl_last]
    ring = [i ^ (i >> 1) for i in range(cols)]
    where_in = [ring.index(i) for i in range(cols)]

    row, col = lax.axis_index("row"), lax.axis_index("col")
    chip, core = lax.div(row, 2), lax.rem(row, 2)
    spot = table(col, where_in)

    def ring_col(step):
        return table(lax.rem(spot + step + cols, cols), ring)

    above, below = (row + 2, col), (row - 2, col)
    sibling = (chip * 2 + 1 - core, col)
    ahead, behind = (row, ring_col(1)), (row, ring_col(-1))
    has_above, has_below = chip < chips - 1, chip > 0
    live = live_slots(row, rows, slots)

    def own_panel(c):
        return pltpu.make_async_copy(
            panel.at[:, :, pl.ds(c * kc, kc)], sl[c].at[pl.ds(row * pan, pan)], load_sem.at[c])

    share = pivot.shape[0] // cols
    own_factor = pltpu.make_async_copy(
        pivot.at[pl.ds(pl.multiple_of(col * share, share), share)], factor.at[core, col, chip], load_sem.at[CHUNKS])
    own_factor.start()
    for c in range(CHUNKS):
        own_panel(c).start()

    def slot_in(t):
        return pltpu.make_async_copy(trailing.at[t], acc.at[t], in_sem.at[t])

    barrier = pltpu.get_barrier_semaphore()
    for other in (sibling, ahead, behind):
        pl.semaphore_signal(barrier, inc=1, device_id=other, device_id_type=MESH)

    @pl.when(has_above)
    def _():
        pl.semaphore_signal(barrier, inc=1, device_id=above, device_id_type=MESH)

    @pl.when(has_below)
    def _():
        pl.semaphore_signal(barrier, inc=1, device_id=below, device_id_type=MESH)

    pl.semaphore_wait(barrier, 3 + jnp.where(has_above, 1, 0) + jnp.where(has_below, 1, 0))

    def remote(ref, send, recv, device):
        return pltpu.make_async_remote_copy(
            src_ref=ref, dst_ref=ref, send_sem=send, recv_sem=recv, device_id=device, device_id_type=MESH)

    def factor_part(side, at, src):
        depth = -(-((src + 1) * block) // kc) * kc
        return factor.at[side, at, src, :, pl.ds(0, depth)]

    def factor_line(up, src):
        return remote(factor_part(core, col, src), lz_send.at[0 if up else 1, src], lz_recv.at[src], above if up else below)

    def factor_ring(fwd, at, src):
        return remote(factor_part(core, at, src), lr_send.at[0 if fwd else 1, at, src], lr_recv.at[at, src], ahead if fwd else behind)

    def factor_sib(side, at, src):
        return remote(factor_part(side, at, src), ls_send.at[at, src], ls_recv.at[at, src], sibling)

    def piece(c, src, side, i):
        first = (src * 2 + side) * pan
        count = PIECES[c]
        if count <= pan:
            return sl[c].at[pl.ds(first + i * (pan // count), pan // count)]
        splits = count // pan
        return sl[c].at[first + i // splits, pl.ds((i % splits) * (height // splits), height // splits)]

    def row_line(c, i, up, src):
        return remote(piece(c, src, core, i), row_send.at[c, i, 0 if up else 1, src], row_recv.at[c, i, src], above if up else below)

    def row_sib(c, i, src, side):
        return remote(piece(c, src, side, i), sib_send.at[c, i, src], sib_recv.at[c, i, src], sibling)

    def q_ring(c, fwd, at, h):
        return remote(q[c].at[h, at], q_send.at[c, 0 if fwd else 1, at, h], q_recv.at[c, at, h], ahead if fwd else behind)

    def goes(d, fwd, h):
        return d < far or (d == far and (h % 2 == 0) == fwd)

    def factor_own():
        for s in range(chips):
            @pl.when(chip == s)
            def _():
                @pl.when(has_above)
                def _():
                    factor_line(True, s).start()

                @pl.when(has_below)
                def _():
                    factor_line(False, s).start()
                factor_spread(s)

    def factor_spread(s):
        for fwd in (True, False):
            if goes(1, fwd, s):
                factor_ring(fwd, col, s).start()
        factor_sib(core, col, s).start()

    def factor_event(d):
        for s in range(chips):
            @pl.when(chip - d == s)
            def _():
                factor_line(True, s).wait_recv()

                @pl.when(has_above)
                def _():
                    factor_line(True, s).start()
                factor_spread(s)

            @pl.when(chip + d == s)
            def _():
                factor_line(False, s).wait_recv()

                @pl.when(has_below)
                def _():
                    factor_line(False, s).start()
                factor_spread(s)

    def factor_ring_event(d):
        for s in range(chips):
            for fwd in (True, False):
                if goes(d, fwd, s):
                    at = ring_col(-d if fwd else d)
                    factor_ring(fwd, at, s).wait_recv()
                    if goes(d + 1, fwd, s):
                        factor_ring(fwd, at, s).start()
                    factor_sib(core, at, s).start()

    def factor_drain():
        for s in range(chips):
            @pl.when(has_above & (chip >= s))
            def _():
                factor_line(True, s).wait_send()

            @pl.when(has_below & (chip <= s))
            def _():
                factor_line(False, s).wait_send()
            for at in range(cols):
                factor_sib(core, at, s).wait_send()
            for d in range(far):
                for fwd in (True, False):
                    if goes(d + 1, fwd, s):
                        factor_ring(fwd, ring_col(-d if fwd else d), s).wait_send()

    def row_own(c, i):
        @pl.when(has_above)
        def _():
            row_line(c, i, True, chip).start()

        @pl.when(has_below)
        def _():
            row_line(c, i, False, chip).start()
        row_sib(c, i, chip, core).start()

    def row_event(c, d):
        for i in range(PIECES[c]):
            @pl.when(chip - d >= 0)
            def _():
                row_line(c, i, True, chip - d).wait_recv()

                @pl.when(has_above)
                def _():
                    row_line(c, i, True, chip - d).start()
                row_sib(c, i, chip - d, core).start()

            @pl.when(chip + d < chips)
            def _():
                row_line(c, i, False, chip + d).wait_recv()

                @pl.when(has_below)
                def _():
                    row_line(c, i, False, chip + d).start()
                row_sib(c, i, chip + d, core).start()

    def row_drain(c):
        for i in range(PIECES[c]):
            @pl.when(has_above)
            def _():
                over(0, chip + 1, lambda src: row_line(c, i, True, src).wait_send())

            @pl.when(has_below)
            def _():
                over(chip, chips, lambda src: row_line(c, i, False, src).wait_send())
            over(0, chips, lambda src: row_sib(c, i, src, core).wait_send())

    def q_event(c, d):
        for h in range(pan):
            for fwd in (True, False):
                if goes(d, fwd, h):
                    at = ring_col(-d if fwd else d)
                    if d > 0:
                        q_ring(c, fwd, at, h).wait_recv()
                    if goes(d + 1, fwd, h):
                        q_ring(c, fwd, at, h).start()

    def q_drain(c):
        for d in range(far):
            for h in range(pan):
                for fwd in (True, False):
                    if goes(d + 1, fwd, h):
                        q_ring(c, fwd, ring_col(-d if fwd else d), h).wait_send()

    own_factor.wait()
    factor_own()
    own_panel(0).wait()
    sent = 0
    for d in range(1, chips):
        if sent < PIECES[0]:
            row_own(0, sent)
            sent += 1
        factor_event(d)
    for i in range(sent, PIECES[0]):
        row_own(0, i)
    for c in range(1, CHUNKS):
        own_panel(c).wait()
        for i in range(PIECES[c]):
            row_own(c, i)
    over(0, slots, lambda t: slot_in(t).start())

    for c in range(CHUNKS):
        hi, lo = halves(sl[c][pl.ds(row * pan, pan)].reshape(pan * height, kc))
        own_hi[:, c * kc:(c + 1) * kc] = hi
        own_lo[:, c * kc:(c + 1) * kc] = lo

    for d in range(1, far + 1):
        factor_ring_event(d)
    for s in range(chips):
        for at in range(cols):
            factor_sib(1 - core, at, s).wait_recv()

    for b in range(chips):
        depth = min(order, -(-((b + 1) * block) // 128) * 128)
        l_hi, l_lo = halves(factor[:, :, b, :, :depth].reshape(block, depth))
        a_hi, a_lo = own_hi[:, :depth], own_lo[:, :depth]
        part = dot_nt(a_hi, l_hi) + (dot_nt(a_hi, l_lo) + dot_nt(a_lo, l_hi))
        solved_buf[:, :, b * block:(b + 1) * block] = part.reshape(pan, height, block)
    for b in range(CHUNKS):
        hi, lo = halves(solved_buf[:, :, b * kc:(b + 1) * kc].reshape(pan * height, kc))
        own_hi[:, b * kc:(b + 1) * kc] = hi
        own_lo[:, b * kc:(b + 1) * kc] = lo

    for c in range(CHUNKS):
        first = (c * kc) // block
        span = pl.ds(c * kc, kc)
        l_rows = jnp.concatenate([factor[:, :, b, :, span].reshape(block, kc) for b in range(first, chips)], axis=0)
        l_hi, l_lo = halves(l_rows)
        s_hi, s_lo = own_hi[:, first * block:], own_lo[:, first * block:]
        part = dot_nn(s_hi, l_hi) + (dot_nn(s_hi, l_lo) + dot_nn(s_lo, l_hi))
        part = part.reshape(pan, height, kc)
        for h in range(pan):
            q[c][h, col] = part[h]
        q_event(c, 0)

    for c in range(CHUNKS):
        row_event(c, 1)
        if c > 0:
            for d in range(1, far):
                q_event(c - 1, d)
    for d in range(2, chips - 1):
        for c in range(CHUNKS):
            row_event(c, d)
            if d == 2 and c == 0:
                for e in range(1, far):
                    q_event(CHUNKS - 1, e)
    for c in range(CHUNKS):
        q_event(c, far)

    over(0, slots, lambda t: slot_in(t).wait())

    def update(c):
        def one(t):
            left = q3[tiles[0, t]]
            r_hi, r_lo = halves(sl[c][tiles[1, t]])
            right = jnp.concatenate([r_hi, r_lo, r_hi], axis=1)
            acc[t] = acc[t] - dot_nt(left, right)
        over(0, live, one)

    for c in range(CHUNKS):
        into = q3 if c < CHUNKS - 1 else q3_last
        for h in range(pan):
            hi, lo = halves(q[c][h].reshape(cols * height, kc))
            into[h, :, 0:kc] = hi
            into[h, :, kc:2 * kc] = hi
            into[h, :, 2 * kc:3 * kc] = lo
        row_event(c, chips - 1)
        for i in range(PIECES[c]):
            over(0, chips, lambda src: row_sib(c, i, src, 1 - core).wait_recv())
        if c < CHUNKS - 1:
            update(c)

    factor_drain()
    for c in range(CHUNKS):
        row_drain(c)
        q_drain(c)


def finish_kernel(rows, solved_buf, acc, q3, right_tiles, tiles, solved, updated,
                  solved_stage, stage, solved_sem, out_sem):
    slots = acc.shape[0]
    live = live_slots(lax.axis_index("row"), rows, slots)
    solved_copy = pltpu.make_async_copy(solved_stage, solved, solved_sem)

    def slot_out(t):
        at = lax.rem(t, STAGES)
        return pltpu.make_async_copy(stage.at[at], updated.at[t], out_sem.at[at])

    def staged(value):
        def one(t):
            @pl.when(t >= STAGES)
            def _():
                slot_out(t - STAGES).wait()

            stage[lax.rem(t, STAGES)] = value(t)
            slot_out(t).start()
        return one

    def touched(t):
        r_hi, r_lo = halves(right_tiles[tiles[1, t]])
        right = jnp.concatenate([r_hi, r_lo, r_hi], axis=1)
        return acc[t] - dot_nt(q3[tiles[0, t]], right)

    over(0, live, staged(touched))
    over(live, slots, staged(lambda t: acc[t]))
    solved_stage[...] = solved_buf[...]
    solved_copy.start()
    over(slots - STAGES, slots, lambda t: slot_out(t).wait())
    solved_copy.wait()


def per_device(rows, cols, pivot_inverse, panel, trailing, tile_list):
    pan, height, order = panel.shape
    slots, _, width = trailing.shape
    chips, kc = rows // 2, order // CHUNKS
    share = pivot_inverse.shape[0] // cols
    most = max(PIECES)
    dma = pltpu.SemaphoreType.DMA
    anywhere = pl.BlockSpec(memory_space=pl.ANY)
    vector = pl.BlockSpec(memory_space=pltpu.VMEM)
    scalar = pl.BlockSpec(memory_space=pltpu.SMEM)
    tiles = tile_list.T
    carried = pl.pallas_call(
        functools.partial(gather_kernel, rows, cols),
        out_shape=(
            pltpu.VMEM(panel.shape, f32),
            pltpu.VMEM(trailing.shape, f32),
            pltpu.VMEM((pan, cols * height, 3 * kc), bf16),
            pltpu.VMEM((rows * pan, height, kc), f32),
        ),
        in_specs=[anywhere, anywhere, anywhere, scalar],
        out_specs=(vector,) * 4,
        scratch_shapes=[
            [pltpu.VMEM((rows * pan, height, kc), f32) for _ in range(CHUNKS - 1)],
            [pltpu.VMEM((pan, cols, height, kc), f32) for _ in range(CHUNKS)],
            pltpu.VMEM((2, cols, chips, share, order), f32),
            pltpu.VMEM((pan * height, order), bf16),
            pltpu.VMEM((pan * height, order), bf16),
            pltpu.VMEM((pan, cols * height, 3 * kc), bf16),
            dma((CHUNKS + 1,)),
            dma((slots,)),
            dma((chips,)),
            dma((2, chips)),
            dma((cols, chips)),
            dma((2, cols, chips)),
            dma((cols, chips)),
            dma((cols, chips)),
            dma((CHUNKS, most, chips)),
            dma((CHUNKS, most, 2, chips)),
            dma((CHUNKS, most, chips)),
            dma((CHUNKS, most, chips)),
            dma((CHUNKS, cols, pan)),
            dma((CHUNKS, 2, cols, pan)),
        ],
        compiler_params=pltpu.CompilerParams(
            collective_id=0, has_side_effects=True, vmem_limit_bytes=34 * 1024 * 1024
        ),
    )(pivot_inverse, panel, trailing, tiles)
    carried = [pltpu.with_memory_space_constraint(x, pltpu.VMEM) for x in carried]
    return pl.pallas_call(
        functools.partial(finish_kernel, rows),
        out_shape=(
            jax.ShapeDtypeStruct(panel.shape, f32),
            jax.ShapeDtypeStruct(trailing.shape, f32),
        ),
        in_specs=[vector, vector, vector, vector, scalar],
        out_specs=(anywhere, anywhere),
        scratch_shapes=[
            pltpu.VMEM(panel.shape, f32),
            pltpu.VMEM((STAGES, order, width), f32),
            dma(()),
            dma((STAGES,)),
        ],
        compiler_params=pltpu.CompilerParams(vmem_limit_bytes=34 * 1024 * 1024),
    )(*carried, tiles)


def solution(mesh):
    placed = (P("row", None), P("row", "col", None), P("row", None, "col"), P("row", None))
    return jax.shard_map(
        functools.partial(per_device, mesh.shape["row"], mesh.shape["col"]),
        mesh=mesh,
        in_specs=placed,
        out_specs=(P("row", "col", None), P("row", None, "col")),
        check_vma=False,
    )
```

```python
import functools

import jax
import jax.numpy as jnp
from jax import lax
from jax.experimental import pallas as pl
from jax.experimental.pallas import tpu as pltpu
from jax.sharding import PartitionSpec as P

MESH = pl.DeviceIdType.MESH
LIGHT = 6
PARTS = (2, 2, 2, 1, 1)
PIECES = (4, 1, 1, 1, 2)
CHUNKS = len(PARTS)
STAGES = 4
f32, bf16 = jnp.float32, jnp.bfloat16


def halves(x):
    hi = x.astype(bf16)
    return hi, (x - hi.astype(f32)).astype(bf16)


def dot_nt(a, b):
    return lax.dot_general(a, b, (((1,), (1,)), ((), ())), preferred_element_type=f32)


def dot_nn(a, b):
    return lax.dot_general(a, b, (((1,), (0,)), ((), ())), preferred_element_type=f32)


def table(index, values):
    found = jnp.int32(0)
    for at, value in enumerate(values):
        found = jnp.where(index == at, jnp.int32(value), found)
    return found


def chunk_spans(order):
    unit = order // sum(PARTS)
    return [(sum(PARTS[:c]) * unit, PARTS[c] * unit) for c in range(CHUNKS)]


def over(lo, hi, act):
    def body(t, carry):
        act(t)
        return carry
    lax.fori_loop(lo, hi, body, 0)


def live_slots(row, rows, slots):
    return jnp.where(row < rows // 2, jnp.int32(min(LIGHT, slots)), jnp.int32(slots))


def gather_kernel(rows, cols, pivot, panel, trailing, tiles,
                  solved_buf, acc, q3_last, sl_last,
                  sl, q, factor, own_hi, own_lo, q3,
                  load_sem, in_sem,
                  lz_recv, lz_send, lr_recv, lr_send, ls_recv, ls_send,
                  row_recv, row_send, sib_recv, sib_send, q_recv, q_send):
    chips = rows // 2
    pan, height, order = panel.shape
    slots = trailing.shape[0]
    spans = chunk_spans(order)
    block = order // chips
    far = cols // 2
    sl = [*sl, sl_last]
    ring = [i ^ (i >> 1) for i in range(cols)]
    where_in = [ring.index(i) for i in range(cols)]

    row, col = lax.axis_index("row"), lax.axis_index("col")
    chip, core = lax.div(row, 2), lax.rem(row, 2)
    spot = table(col, where_in)

    def ring_col(step):
        return table(lax.rem(spot + step + cols, cols), ring)

    above, below = (row + 2, col), (row - 2, col)
    sibling = (chip * 2 + 1 - core, col)
    ahead, behind = (row, ring_col(1)), (row, ring_col(-1))
    has_above, has_below = chip < chips - 1, chip > 0
    live = live_slots(row, rows, slots)

    def own_panel(c):
        return pltpu.make_async_copy(
            panel.at[:, :, pl.ds(*spans[c])], sl[c].at[pl.ds(row * pan, pan)], load_sem.at[c])

    share = pivot.shape[0] // cols
    own_factor = pltpu.make_async_copy(
        pivot.at[pl.ds(pl.multiple_of(col * share, share), share)], factor.at[core, col, chip], load_sem.at[CHUNKS])
    own_factor.start()
    for c in range(CHUNKS):
        own_panel(c).start()

    def slot_in(t):
        return pltpu.make_async_copy(trailing.at[t], acc.at[t], in_sem.at[t])

    barrier = pltpu.get_barrier_semaphore()
    for other in (sibling, ahead, behind):
        pl.semaphore_signal(barrier, inc=1, device_id=other, device_id_type=MESH)

    @pl.when(has_above)
    def _():
        pl.semaphore_signal(barrier, inc=1, device_id=above, device_id_type=MESH)

    @pl.when(has_below)
    def _():
        pl.semaphore_signal(barrier, inc=1, device_id=below, device_id_type=MESH)

    pl.semaphore_wait(barrier, 3 + jnp.where(has_above, 1, 0) + jnp.where(has_below, 1, 0))

    def remote(ref, send, recv, device):
        return pltpu.make_async_remote_copy(
            src_ref=ref, dst_ref=ref, send_sem=send, recv_sem=recv, device_id=device, device_id_type=MESH)

    def reach(b):
        return min(at + kc for at, kc in spans if at + kc >= (b + 1) * block)

    def factor_part(side, at, src):
        depth = reach(src)
        return factor.at[side, at, src, :, pl.ds(0, depth)]

    def factor_line(up, src):
        return remote(factor_part(core, col, src), lz_send.at[0 if up else 1, src], lz_recv.at[src], above if up else below)

    def factor_ring(fwd, at, src):
        return remote(factor_part(core, at, src), lr_send.at[0 if fwd else 1, at, src], lr_recv.at[at, src], ahead if fwd else behind)

    def factor_sib(side, at, src):
        return remote(factor_part(side, at, src), ls_send.at[at, src], ls_recv.at[at, src], sibling)

    def piece(c, src, side, i):
        first = (src * 2 + side) * pan
        count = PIECES[c]
        if count <= pan:
            return sl[c].at[pl.ds(first + i * (pan // count), pan // count)]
        splits = count // pan
        return sl[c].at[first + i // splits, pl.ds((i % splits) * (height // splits), height // splits)]

    def row_line(c, i, up, src):
        return remote(piece(c, src, core, i), row_send.at[c, i, 0 if up else 1, src], row_recv.at[c, i, src], above if up else below)

    def row_sib(c, i, src, side):
        return remote(piece(c, src, side, i), sib_send.at[c, i, src], sib_recv.at[c, i, src], sibling)

    def q_ring(c, fwd, at, h):
        return remote(q[c].at[h, at], q_send.at[c, 0 if fwd else 1, at, h], q_recv.at[c, at, h], ahead if fwd else behind)

    def goes(d, fwd, h):
        return d < far or (d == far and (h % 2 == 0) == fwd)

    def factor_own():
        for s in range(chips):
            @pl.when(chip == s)
            def _():
                @pl.when(has_above)
                def _():
                    factor_line(True, s).start()

                @pl.when(has_below)
                def _():
                    factor_line(False, s).start()
                factor_spread(s)

    def factor_spread(s):
        for fwd in (True, False):
            if goes(1, fwd, s):
                factor_ring(fwd, col, s).start()
        factor_sib(core, col, s).start()

    def factor_event(d):
        for s in range(chips):
            @pl.when(chip - d == s)
            def _():
                factor_line(True, s).wait_recv()

                @pl.when(has_above)
                def _():
                    factor_line(True, s).start()
                factor_spread(s)

            @pl.when(chip + d == s)
            def _():
                factor_line(False, s).wait_recv()

                @pl.when(has_below)
                def _():
                    factor_line(False, s).start()
                factor_spread(s)

    def factor_ring_event(d):
        for s in range(chips):
            for fwd in (True, False):
                if goes(d, fwd, s):
                    at = ring_col(-d if fwd else d)
                    factor_ring(fwd, at, s).wait_recv()
                    if goes(d + 1, fwd, s):
                        factor_ring(fwd, at, s).start()
                    factor_sib(core, at, s).start()

    def factor_drain():
        for s in range(chips):
            @pl.when(has_above & (chip >= s))
            def _():
                factor_line(True, s).wait_send()

            @pl.when(has_below & (chip <= s))
            def _():
                factor_line(False, s).wait_send()
            for at in range(cols):
                factor_sib(core, at, s).wait_send()
            for d in range(far):
                for fwd in (True, False):
                    if goes(d + 1, fwd, s):
                        factor_ring(fwd, ring_col(-d if fwd else d), s).wait_send()

    def row_own(c, i):
        @pl.when(has_above)
        def _():
            row_line(c, i, True, chip).start()

        @pl.when(has_below)
        def _():
            row_line(c, i, False, chip).start()
        row_sib(c, i, chip, core).start()

    def row_event(c, d, relay):
        for i in range(PIECES[c]):
            @pl.when((chip - d >= 0) & (has_above if relay else ~has_above))
            def _():
                row_line(c, i, True, chip - d).wait_recv()
                if relay:
                    row_line(c, i, True, chip - d).start()
                row_sib(c, i, chip - d, core).start()

            @pl.when((chip + d < chips) & (has_below if relay else ~has_below))
            def _():
                row_line(c, i, False, chip + d).wait_recv()
                if relay:
                    row_line(c, i, False, chip + d).start()
                row_sib(c, i, chip + d, core).start()

    def row_drain(c):
        for i in range(PIECES[c]):
            @pl.when(has_above)
            def _():
                over(0, chip + 1, lambda src: row_line(c, i, True, src).wait_send())

            @pl.when(has_below)
            def _():
                over(chip, chips, lambda src: row_line(c, i, False, src).wait_send())
            over(0, chips, lambda src: row_sib(c, i, src, core).wait_send())

    def q_event(c, d):
        for h in range(pan):
            for fwd in (True, False):
                if goes(d, fwd, h):
                    at = ring_col(-d if fwd else d)
                    if d > 0:
                        q_ring(c, fwd, at, h).wait_recv()
                    if goes(d + 1, fwd, h):
                        q_ring(c, fwd, at, h).start()

    def q_drain(c):
        for d in range(far):
            for h in range(pan):
                for fwd in (True, False):
                    if goes(d + 1, fwd, h):
                        q_ring(c, fwd, ring_col(-d if fwd else d), h).wait_send()

    own_factor.wait()
    factor_own()
    own_panel(0).wait()
    sent = 0
    for d in range(1, chips):
        if sent < PIECES[0]:
            row_own(0, sent)
            sent += 1
        factor_event(d)
    for i in range(sent, PIECES[0]):
        row_own(0, i)

    def own_send(c):
        for i in range(PIECES[c]):
            row_own(c, i)

    for c in range(1, CHUNKS):
        own_panel(c).wait()
        if c < 3:
            own_send(c)
    over(0, slots, lambda t: slot_in(t).start())

    for c, (at, kc) in enumerate(spans):
        hi, lo = halves(sl[c][pl.ds(row * pan, pan)].reshape(pan * height, kc))
        own_hi[:, at:at + kc] = hi
        own_lo[:, at:at + kc] = lo

    for d in range(1, far + 1):
        factor_ring_event(d)
    for s in range(chips):
        for at in range(cols):
            factor_sib(1 - core, at, s).wait_recv()

    for b in range(chips):
        depth = reach(b)
        l_hi, l_lo = halves(factor[:, :, b, :, :depth].reshape(block, depth))
        a_hi, a_lo = own_hi[:, :depth], own_lo[:, :depth]
        part = dot_nt(a_hi, l_hi) + (dot_nt(a_hi, l_lo) + dot_nt(a_lo, l_hi))
        solved_buf[:, :, b * block:(b + 1) * block] = part.reshape(pan, height, block)
    for at, kc in spans:
        hi, lo = halves(solved_buf[:, :, at:at + kc].reshape(pan * height, kc))
        own_hi[:, at:at + kc] = hi
        own_lo[:, at:at + kc] = lo

    for c, (at, kc) in enumerate(spans):
        first = at // block
        l_rows = jnp.concatenate([factor[:, :, b, :, at:at + kc].reshape(block, kc) for b in range(first, chips)], axis=0)
        l_hi, l_lo = halves(l_rows)
        s_hi, s_lo = own_hi[:, first * block:], own_lo[:, first * block:]
        part = dot_nn(s_hi, l_hi) + (dot_nn(s_hi, l_lo) + dot_nn(s_lo, l_hi))
        part = part.reshape(pan, height, kc)
        for h in range(pan):
            q[c][h, col] = part[h]
        q_event(c, 0)

    def q_relay(c):
        for d in range(1, far):
            q_event(c, d)

    def update(c):
        kc = spans[c][1]

        def one(t):
            left = q3[tiles[0, t], :, 0:3 * kc]
            r_hi, r_lo = halves(sl[c][tiles[1, t]])
            right = jnp.concatenate([r_hi, r_lo, r_hi], axis=1)
            acc[t] = acc[t] - dot_nt(left, right)
        over(0, live, one)

    def complete(c):
        q_event(c, far)
        kc = spans[c][1]
        into = q3 if c < CHUNKS - 1 else q3_last
        for h in range(pan):
            hi, lo = halves(q[c][h].reshape(cols * height, kc))
            into[h, :, 0:kc] = hi
            into[h, :, kc:2 * kc] = hi
            into[h, :, 2 * kc:3 * kc] = lo
        for d in range(1, chips):
            row_event(c, d, False)
        for i in range(PIECES[c]):
            over(0, chips, lambda src: row_sib(c, i, src, 1 - core).wait_recv())

    row_event(0, 1, True)
    row_event(1, 1, True)
    q_relay(0)
    for d in range(2, chips - 1):
        row_event(0, d, True)
        if d == 2:
            q_relay(1)
        row_event(1, d, True)
    own_send(3)
    own_send(4)
    q_relay(2)
    for d in range(1, chips - 1):
        row_event(2, d, True)
        if d == 1:
            q_relay(3)
            q_relay(4)
    for c in (3, 4):
        for d in range(1, chips - 1):
            row_event(c, d, True)
    over(0, slots, lambda t: slot_in(t).wait())
    for c in range(CHUNKS - 1):
        complete(c)
        update(c)
    complete(CHUNKS - 1)

    factor_drain()
    for c in range(CHUNKS):
        row_drain(c)
        q_drain(c)


def finish_kernel(rows, solved_buf, acc, q3, right_tiles, tiles, solved, updated,
                  stage, solved_sem, rest_sem, out_sem):
    slots = acc.shape[0]
    live = live_slots(lax.axis_index("row"), rows, slots)
    solved_copy = pltpu.make_async_copy(solved_buf, solved, solved_sem)

    def rest_out(t):
        return pltpu.make_async_copy(acc.at[t], updated.at[t], rest_sem.at[t])

    def slot_out(t):
        at = lax.rem(t, STAGES)
        return pltpu.make_async_copy(stage.at[at], updated.at[t], out_sem.at[at])

    over(live, slots, lambda t: rest_out(t).start())
    solved_copy.start()

    def one(t):
        @pl.when(t >= STAGES)
        def _():
            slot_out(t - STAGES).wait()

        r_hi, r_lo = halves(right_tiles[tiles[1, t]])
        right = jnp.concatenate([r_hi, r_lo, r_hi], axis=1)
        stage[lax.rem(t, STAGES)] = acc[t] - dot_nt(q3[tiles[0, t]], right)
        slot_out(t).start()

    over(0, live, one)
    over(live, slots, lambda t: rest_out(t).wait())
    over(live - STAGES, live, lambda t: slot_out(t).wait())
    solved_copy.wait()


def per_device(rows, cols, pivot_inverse, panel, trailing, tile_list):
    pan, height, order = panel.shape
    slots, _, width = trailing.shape
    chips = rows // 2
    widths = [kc for _, kc in chunk_spans(order)]
    share = pivot_inverse.shape[0] // cols
    most = max(PIECES)
    dma = pltpu.SemaphoreType.DMA
    anywhere = pl.BlockSpec(memory_space=pl.ANY)
    vector = pl.BlockSpec(memory_space=pltpu.VMEM)
    scalar = pl.BlockSpec(memory_space=pltpu.SMEM)
    tiles = tile_list.T
    carried = pl.pallas_call(
        functools.partial(gather_kernel, rows, cols),
        out_shape=(
            pltpu.VMEM(panel.shape, f32),
            pltpu.VMEM(trailing.shape, f32),
            pltpu.VMEM((pan, cols * height, 3 * widths[-1]), bf16),
            pltpu.VMEM((rows * pan, height, widths[-1]), f32),
        ),
        in_specs=[anywhere, anywhere, anywhere, scalar],
        out_specs=(vector,) * 4,
        scratch_shapes=[
            [pltpu.VMEM((rows * pan, height, kc), f32) for kc in widths[:-1]],
            [pltpu.VMEM((pan, cols, height, kc), f32) for kc in widths],
            pltpu.VMEM((2, cols, chips, share, order), f32),
            pltpu.VMEM((pan * height, order), bf16),
            pltpu.VMEM((pan * height, order), bf16),
            pltpu.VMEM((pan, cols * height, 3 * max(widths)), bf16),
            dma((CHUNKS + 1,)),
            dma((slots,)),
            dma((chips,)),
            dma((2, chips)),
            dma((cols, chips)),
            dma((2, cols, chips)),
            dma((cols, chips)),
            dma((cols, chips)),
            dma((CHUNKS, most, chips)),
            dma((CHUNKS, most, 2, chips)),
            dma((CHUNKS, most, chips)),
            dma((CHUNKS, most, chips)),
            dma((CHUNKS, cols, pan)),
            dma((CHUNKS, 2, cols, pan)),
        ],
        compiler_params=pltpu.CompilerParams(
            collective_id=0, has_side_effects=True, vmem_limit_bytes=36 * 1024 * 1024
        ),
    )(pivot_inverse, panel, trailing, tiles)
    carried = [pltpu.with_memory_space_constraint(x, pltpu.VMEM) for x in carried]
    return pl.pallas_call(
        functools.partial(finish_kernel, rows),
        out_shape=(
            jax.ShapeDtypeStruct(panel.shape, f32),
            jax.ShapeDtypeStruct(trailing.shape, f32),
        ),
        in_specs=[vector, vector, vector, vector, scalar],
        out_specs=(anywhere, anywhere),
        scratch_shapes=[
            pltpu.VMEM((STAGES, order, width), f32),
            dma(()),
            dma((slots,)),
            dma((STAGES,)),
        ],
        compiler_params=pltpu.CompilerParams(vmem_limit_bytes=36 * 1024 * 1024),
    )(*carried, tiles)


def solution(mesh):
    placed = (P("row", None), P("row", "col", None), P("row", None, "col"), P("row", None))
    return jax.shard_map(
        functools.partial(per_device, mesh.shape["row"], mesh.shape["col"]),
        mesh=mesh,
        in_specs=placed,
        out_specs=(P("row", "col", None), P("row", None, "col")),
        check_vma=False,
    )
```

```python
import functools

import jax
import jax.numpy as jnp
from jax import lax
from jax.experimental import pallas as pl
from jax.experimental.pallas import tpu as pltpu
from jax.sharding import PartitionSpec as P

MESH = pl.DeviceIdType.MESH
LIGHT = 6
PARTS = (2, 2, 2, 1, 1)
PIECES = (4, 1, 1, 1, 2)
CHUNKS = len(PARTS)
STAGES = 4
f32, bf16 = jnp.float32, jnp.bfloat16


def halves(x):
    hi = x.astype(bf16)
    return hi, (x - hi.astype(f32)).astype(bf16)


def dot_nt(a, b):
    return lax.dot_general(a, b, (((1,), (1,)), ((), ())), preferred_element_type=f32)


def dot_nn(a, b):
    return lax.dot_general(a, b, (((1,), (0,)), ((), ())), preferred_element_type=f32)


def table(index, values):
    found = jnp.int32(0)
    for at, value in enumerate(values):
        found = jnp.where(index == at, jnp.int32(value), found)
    return found


def chunk_spans(order):
    unit = order // sum(PARTS)
    return [(sum(PARTS[:c]) * unit, PARTS[c] * unit) for c in range(CHUNKS)]


def over(lo, hi, act):
    def body(t, carry):
        act(t)
        return carry
    lax.fori_loop(lo, hi, body, 0)


def live_slots(row, rows, slots):
    return jnp.where(row < rows // 2, jnp.int32(min(LIGHT, slots)), jnp.int32(slots))


def gather_kernel(rows, cols, pivot, panel, trailing, tiles,
                  solved_buf, acc, q3_last, sl_last,
                  sl, q, factor, own_hi, own_lo, q3,
                  load_sem, in_sem,
                  lz_recv, lz_send, lr_recv, lr_send, ls_recv, ls_send,
                  row_recv, row_send, sib_recv, sib_send, q_recv, q_send):
    chips = rows // 2
    pan, height, order = panel.shape
    slots = trailing.shape[0]
    spans = chunk_spans(order)
    block = order // chips
    far = cols // 2
    sl = [*sl, sl_last]
    ring = [i ^ (i >> 1) for i in range(cols)]
    where_in = [ring.index(i) for i in range(cols)]

    row, col = lax.axis_index("row"), lax.axis_index("col")
    chip, core = lax.div(row, 2), lax.rem(row, 2)
    spot = table(col, where_in)

    def ring_col(step):
        return table(lax.rem(spot + step + cols, cols), ring)

    above, below = (row + 2, col), (row - 2, col)
    sibling = (chip * 2 + 1 - core, col)
    ahead, behind = (row, ring_col(1)), (row, ring_col(-1))
    has_above, has_below = chip < chips - 1, chip > 0
    live = live_slots(row, rows, slots)

    def own_panel(c):
        return pltpu.make_async_copy(
            panel.at[:, :, pl.ds(*spans[c])], sl[c].at[pl.ds(row * pan, pan)], load_sem.at[c])

    share = pivot.shape[0] // cols
    own_factor = pltpu.make_async_copy(
        pivot.at[pl.ds(pl.multiple_of(col * share, share), share)], factor.at[core, col, chip], load_sem.at[CHUNKS])
    own_factor.start()
    for c in range(CHUNKS):
        own_panel(c).start()

    def slot_in(t):
        return pltpu.make_async_copy(trailing.at[t], acc.at[t], in_sem.at[t])

    barrier = pltpu.get_barrier_semaphore()
    for other in (sibling, ahead, behind):
        pl.semaphore_signal(barrier, inc=1, device_id=other, device_id_type=MESH)

    @pl.when(has_above)
    def _():
        pl.semaphore_signal(barrier, inc=1, device_id=above, device_id_type=MESH)

    @pl.when(has_below)
    def _():
        pl.semaphore_signal(barrier, inc=1, device_id=below, device_id_type=MESH)

    pl.semaphore_wait(barrier, 3 + jnp.where(has_above, 1, 0) + jnp.where(has_below, 1, 0))

    def remote(ref, send, recv, device):
        return pltpu.make_async_remote_copy(
            src_ref=ref, dst_ref=ref, send_sem=send, recv_sem=recv, device_id=device, device_id_type=MESH)

    def reach(b):
        return min(at + kc for at, kc in spans if at + kc >= (b + 1) * block)

    def factor_part(side, at, src):
        depth = reach(src)
        return factor.at[side, at, src, :, pl.ds(0, depth)]

    def factor_line(up, src):
        return remote(factor_part(core, col, src), lz_send.at[0 if up else 1, src], lz_recv.at[src], above if up else below)

    def factor_ring(fwd, at, src):
        return remote(factor_part(core, at, src), lr_send.at[0 if fwd else 1, at, src], lr_recv.at[at, src], ahead if fwd else behind)

    def factor_sib(side, at, src):
        return remote(factor_part(side, at, src), ls_send.at[at, src], ls_recv.at[at, src], sibling)

    def piece(c, src, side, i):
        first = (src * 2 + side) * pan
        count = PIECES[c]
        if count <= pan:
            return sl[c].at[pl.ds(first + i * (pan // count), pan // count)]
        splits = count // pan
        return sl[c].at[first + i // splits, pl.ds((i % splits) * (height // splits), height // splits)]

    def row_line(c, i, up, src):
        return remote(piece(c, src, core, i), row_send.at[c, i, 0 if up else 1, src], row_recv.at[c, i, src], above if up else below)

    def row_sib(c, i, src, side):
        return remote(piece(c, src, side, i), sib_send.at[c, i, src], sib_recv.at[c, i, src], sibling)

    def q_ring(c, fwd, at, h):
        return remote(q[c].at[h, at], q_send.at[c, 0 if fwd else 1, at, h], q_recv.at[c, at, h], ahead if fwd else behind)

    def goes(d, fwd, h):
        return d < far or (d == far and (h % 2 == 0) == fwd)

    def factor_own():
        for s in range(chips):
            @pl.when(chip == s)
            def _():
                @pl.when(has_above)
                def _():
                    factor_line(True, s).start()

                @pl.when(has_below)
                def _():
                    factor_line(False, s).start()
                factor_spread(s)

    def factor_spread(s):
        for fwd in (True, False):
            if goes(1, fwd, s):
                factor_ring(fwd, col, s).start()
        factor_sib(core, col, s).start()

    def factor_event(d):
        for s in range(chips):
            @pl.when(chip - d == s)
            def _():
                factor_line(True, s).wait_recv()

                @pl.when(has_above)
                def _():
                    factor_line(True, s).start()
                factor_spread(s)

            @pl.when(chip + d == s)
            def _():
                factor_line(False, s).wait_recv()

                @pl.when(has_below)
                def _():
                    factor_line(False, s).start()
                factor_spread(s)

    def factor_ring_event(d):
        for s in range(chips):
            for fwd in (True, False):
                if goes(d, fwd, s):
                    at = ring_col(-d if fwd else d)
                    factor_ring(fwd, at, s).wait_recv()
                    if goes(d + 1, fwd, s):
                        factor_ring(fwd, at, s).start()
                    factor_sib(core, at, s).start()

    def factor_drain():
        for s in range(chips):
            @pl.when(has_above & (chip >= s))
            def _():
                factor_line(True, s).wait_send()

            @pl.when(has_below & (chip <= s))
            def _():
                factor_line(False, s).wait_send()
            for at in range(cols):
                factor_sib(core, at, s).wait_send()
            for d in range(far):
                for fwd in (True, False):
                    if goes(d + 1, fwd, s):
                        factor_ring(fwd, ring_col(-d if fwd else d), s).wait_send()

    def row_own(c, i):
        @pl.when(has_above)
        def _():
            row_line(c, i, True, chip).start()

        @pl.when(has_below)
        def _():
            row_line(c, i, False, chip).start()
        row_sib(c, i, chip, core).start()

    def row_event(c, d, relay):
        for i in range(PIECES[c]):
            @pl.when((chip - d >= 0) & (has_above if relay else ~has_above))
            def _():
                row_line(c, i, True, chip - d).wait_recv()
                if relay:
                    row_line(c, i, True, chip - d).start()
                row_sib(c, i, chip - d, core).start()

            @pl.when((chip + d < chips) & (has_below if relay else ~has_below))
            def _():
                row_line(c, i, False, chip + d).wait_recv()
                if relay:
                    row_line(c, i, False, chip + d).start()
                row_sib(c, i, chip + d, core).start()

    def row_drain(c):
        for i in range(PIECES[c]):
            @pl.when(has_above)
            def _():
                over(0, chip + 1, lambda src: row_line(c, i, True, src).wait_send())

            @pl.when(has_below)
            def _():
                over(chip, chips, lambda src: row_line(c, i, False, src).wait_send())
            over(0, chips, lambda src: row_sib(c, i, src, core).wait_send())

    def q_event(c, d):
        for h in range(pan):
            for fwd in (True, False):
                if goes(d, fwd, h):
                    at = ring_col(-d if fwd else d)
                    if d > 0:
                        q_ring(c, fwd, at, h).wait_recv()
                    if goes(d + 1, fwd, h):
                        q_ring(c, fwd, at, h).start()

    def q_drain(c):
        for d in range(far):
            for h in range(pan):
                for fwd in (True, False):
                    if goes(d + 1, fwd, h):
                        q_ring(c, fwd, ring_col(-d if fwd else d), h).wait_send()

    own_factor.wait()
    factor_own()
    own_panel(0).wait()
    sent = 0
    for d in range(1, chips):
        if sent < PIECES[0]:
            row_own(0, sent)
            sent += 1
        factor_event(d)
    for i in range(sent, PIECES[0]):
        row_own(0, i)

    def own_send(c):
        for i in range(PIECES[c]):
            row_own(c, i)

    for c in range(1, CHUNKS):
        own_panel(c).wait()
        if c < 3:
            own_send(c)
    over(0, slots, lambda t: slot_in(t).start())

    for c, (at, kc) in enumerate(spans):
        hi, lo = halves(sl[c][pl.ds(row * pan, pan)].reshape(pan * height, kc))
        own_hi[:, at:at + kc] = hi
        own_lo[:, at:at + kc] = lo

    for d in range(1, far + 1):
        factor_ring_event(d)
    for s in range(chips):
        for at in range(cols):
            factor_sib(1 - core, at, s).wait_recv()

    for b in range(chips):
        depth = reach(b)
        l_hi, l_lo = halves(factor[:, :, b, :, :depth].reshape(block, depth))
        a_hi, a_lo = own_hi[:, :depth], own_lo[:, :depth]
        part = dot_nt(a_hi, l_hi) + (dot_nt(a_hi, l_lo) + dot_nt(a_lo, l_hi))
        solved_buf[:, :, b * block:(b + 1) * block] = part.reshape(pan, height, block)
    for at, kc in spans:
        hi, lo = halves(solved_buf[:, :, at:at + kc].reshape(pan * height, kc))
        own_hi[:, at:at + kc] = hi
        own_lo[:, at:at + kc] = lo

    for c, (at, kc) in enumerate(spans):
        first = at // block
        l_rows = jnp.concatenate([factor[:, :, b, :, at:at + kc].reshape(block, kc) for b in range(first, chips)], axis=0)
        l_hi, l_lo = halves(l_rows)
        s_hi, s_lo = own_hi[:, first * block:], own_lo[:, first * block:]
        part = dot_nn(s_hi, l_hi) + (dot_nn(s_hi, l_lo) + dot_nn(s_lo, l_hi))
        part = part.reshape(pan, height, kc)
        for h in range(pan):
            q[c][h, col] = part[h]
        q_event(c, 0)

    def q_relay(c):
        for d in range(1, far):
            q_event(c, d)

    def update(c):
        kc = spans[c][1]

        def one(t):
            left = q3[tiles[0, t], :, 0:3 * kc]
            r_hi, r_lo = halves(sl[c][tiles[1, t]])
            right = jnp.concatenate([r_hi, r_lo, r_hi], axis=1)
            acc[t] = acc[t] - dot_nt(left, right)
        over(0, live, one)

    def complete(c):
        q_event(c, far)
        kc = spans[c][1]
        into = q3 if c < CHUNKS - 1 else q3_last
        for h in range(pan):
            hi, lo = halves(q[c][h].reshape(cols * height, kc))
            into[h, :, 0:kc] = hi
            into[h, :, kc:2 * kc] = hi
            into[h, :, 2 * kc:3 * kc] = lo
        for d in range(1, chips):
            row_event(c, d, False)
        for i in range(PIECES[c]):
            over(0, chips, lambda src: row_sib(c, i, src, 1 - core).wait_recv())

    row_event(0, 1, True)
    row_event(1, 1, True)
    q_relay(0)
    for d in range(2, chips - 1):
        row_event(0, d, True)
        if d == 2:
            q_relay(1)
        row_event(1, d, True)
    q_relay(2)
    for d in range(1, chips - 1):
        row_event(2, d, True)
    middle = has_above & has_below
    own_send(3)

    @pl.when(~middle)
    def _():
        own_send(4)

    q_relay(3)
    q_relay(4)
    for d in range(1, chips - 1):
        row_event(3, d, True)
    over(0, slots, lambda t: slot_in(t).wait())
    complete(0)
    update(0)

    @pl.when(middle)
    def _():
        own_send(4)

    for d in range(1, chips - 1):
        row_event(4, d, True)
    for c in range(1, CHUNKS - 1):
        complete(c)
        update(c)
    complete(CHUNKS - 1)

    factor_drain()
    for c in range(CHUNKS):
        row_drain(c)
        q_drain(c)


def finish_kernel(rows, solved_buf, acc, q3, right_tiles, tiles, solved, updated,
                  stage, solved_sem, rest_sem, out_sem):
    slots = acc.shape[0]
    live = live_slots(lax.axis_index("row"), rows, slots)
    solved_copy = pltpu.make_async_copy(solved_buf, solved, solved_sem)

    def rest_out(t):
        return pltpu.make_async_copy(acc.at[t], updated.at[t], rest_sem.at[t])

    def slot_out(t):
        at = lax.rem(t, STAGES)
        return pltpu.make_async_copy(stage.at[at], updated.at[t], out_sem.at[at])

    over(live, slots, lambda t: rest_out(t).start())
    solved_copy.start()

    def one(t):
        @pl.when(t >= STAGES)
        def _():
            slot_out(t - STAGES).wait()

        r_hi, r_lo = halves(right_tiles[tiles[1, t]])
        right = jnp.concatenate([r_hi, r_lo, r_hi], axis=1)
        stage[lax.rem(t, STAGES)] = acc[t] - dot_nt(q3[tiles[0, t]], right)
        slot_out(t).start()

    over(0, live, one)
    over(live, slots, lambda t: rest_out(t).wait())
    over(live - STAGES, live, lambda t: slot_out(t).wait())
    solved_copy.wait()


def per_device(rows, cols, pivot_inverse, panel, trailing, tile_list):
    pan, height, order = panel.shape
    slots, _, width = trailing.shape
    chips = rows // 2
    widths = [kc for _, kc in chunk_spans(order)]
    share = pivot_inverse.shape[0] // cols
    most = max(PIECES)
    dma = pltpu.SemaphoreType.DMA
    anywhere = pl.BlockSpec(memory_space=pl.ANY)
    vector = pl.BlockSpec(memory_space=pltpu.VMEM)
    scalar = pl.BlockSpec(memory_space=pltpu.SMEM)
    tiles = tile_list.T
    carried = pl.pallas_call(
        functools.partial(gather_kernel, rows, cols),
        out_shape=(
            pltpu.VMEM(panel.shape, f32),
            pltpu.VMEM(trailing.shape, f32),
            pltpu.VMEM((pan, cols * height, 3 * widths[-1]), bf16),
            pltpu.VMEM((rows * pan, height, widths[-1]), f32),
        ),
        in_specs=[anywhere, anywhere, anywhere, scalar],
        out_specs=(vector,) * 4,
        scratch_shapes=[
            [pltpu.VMEM((rows * pan, height, kc), f32) for kc in widths[:-1]],
            [pltpu.VMEM((pan, cols, height, kc), f32) for kc in widths],
            pltpu.VMEM((2, cols, chips, share, order), f32),
            pltpu.VMEM((pan * height, order), bf16),
            pltpu.VMEM((pan * height, order), bf16),
            pltpu.VMEM((pan, cols * height, 3 * max(widths)), bf16),
            dma((CHUNKS + 1,)),
            dma((slots,)),
            dma((chips,)),
            dma((2, chips)),
            dma((cols, chips)),
            dma((2, cols, chips)),
            dma((cols, chips)),
            dma((cols, chips)),
            dma((CHUNKS, most, chips)),
            dma((CHUNKS, most, 2, chips)),
            dma((CHUNKS, most, chips)),
            dma((CHUNKS, most, chips)),
            dma((CHUNKS, cols, pan)),
            dma((CHUNKS, 2, cols, pan)),
        ],
        compiler_params=pltpu.CompilerParams(
            collective_id=0, has_side_effects=True, vmem_limit_bytes=36 * 1024 * 1024
        ),
    )(pivot_inverse, panel, trailing, tiles)
    carried = [pltpu.with_memory_space_constraint(x, pltpu.VMEM) for x in carried]
    return pl.pallas_call(
        functools.partial(finish_kernel, rows),
        out_shape=(
            jax.ShapeDtypeStruct(panel.shape, f32),
            jax.ShapeDtypeStruct(trailing.shape, f32),
        ),
        in_specs=[vector, vector, vector, vector, scalar],
        out_specs=(anywhere, anywhere),
        scratch_shapes=[
            pltpu.VMEM((STAGES, order, width), f32),
            dma(()),
            dma((slots,)),
            dma((STAGES,)),
        ],
        compiler_params=pltpu.CompilerParams(vmem_limit_bytes=36 * 1024 * 1024),
    )(*carried, tiles)


def solution(mesh):
    placed = (P("row", None), P("row", "col", None), P("row", None, "col"), P("row", None))
    return jax.shard_map(
        functools.partial(per_device, mesh.shape["row"], mesh.shape["col"]),
        mesh=mesh,
        in_specs=placed,
        out_specs=(P("row", "col", None), P("row", None, "col")),
        check_vma=False,
    )
```
